128 devices in a mesh: rack: 64 (over y, z, x_hi, core), queue: 2 (over x_lo).
Axes of the slice: x: 4 (x_hi: 2, x_lo: 2; x = x_hi * 2 + x_lo), y: 4, z: 4, core: 2. Of those that a mesh axis runs over, the one named last changes fastest.
Arguments:
- state: float32 [4096, 4096], P('rack', 'queue'), may hold values from -6 to 6
- queue_blocks: float32 [16, 3, 256, 256], P('queue'), may hold values from -0.21875 to 0.21875
- queue_rows: int32 [16, 3], P('queue'), may hold values from 0 to 15, as said below
- kill_blocks: float32 [16, 3, 256, 256], P('queue'), may hold values from -0.21875 to 0.21875
- kill_rows: int32 [16, 3], P('queue'), may hold values from 0 to 15, as said below
- rate_index: int32 [12], replicated, may hold values from 0 to 7
- rate_table: float32 [8, 2], replicated, may hold values from 0.1 to 2
Outputs:
- advanced: float32 [4096, 4096], P('rack', 'queue')
The draws below stay inside these ranges and needn't reach their ends.
Inputs may be any that keep to these rules, and one draw needn't show every extreme that they name: `queue_rows`: column block c's first row block is c, and its three row blocks are distinct. `kill_rows`: column block c's first row block is c, and its three row blocks are distinct.
All inputs are finite; a program needn't handle non-finite values.
Results may differ from the reference program's by a relative error of at most 0.0001.
Values sent between devices are 32-bit elements; how exact they have to be, the bound alone decides.
A program may use at most 128 MiB of HBM per device.

```python
import math
import jax
import jax.numpy as jnp
from jax import lax

Q = 4096
BS = 256
NRATES = 8
STEPS = 2
QB = 16
RACKS = 12
PATTERNS = 4096


def rows_for(key):
    count = Q // BS
    first = jnp.arange(count, dtype=jnp.int32)
    key_one, key_two = jax.random.split(key)
    step_one = jax.random.randint(key_one, (count,), 1, count // 2, dtype=jnp.int32)
    later = jax.random.randint(key_two, (count,), 1, count - step_one, dtype=jnp.int32)
    second = (first + step_one) % count
    third = (first + step_one + later) % count
    return jnp.stack((first, second, third), axis=1).astype(jnp.int32)


def draw_queue_rows(key, part):
    return rows_for(jax.random.fold_in(key, 3))


def draw_kill_rows(key, part):
    return rows_for(jax.random.fold_in(key, 7))


def plant(drawn, rng, least, largest):
    spot = [jax.random.randint(jax.random.fold_in(rng, axis), (), 0, length) for axis, length in enumerate(drawn.shape)]
    longest = drawn.shape.index(max(drawn.shape))
    beside = spot[:longest] + [(spot[longest] + 1) % drawn.shape[longest]] + spot[longest + 1:]
    return drawn.at[tuple(spot)].set(least).at[tuple(beside)].set(largest)


def steps_of(key, dims, cuts, low, largest):
    factor_of = 1.0
    for position, blocks in cuts:
        heights = jax.random.uniform(jax.random.fold_in(jax.random.fold_in(key, 6), position), (blocks,), jnp.float32, low / len(cuts), largest / len(cuts))
        factor_of = factor_of * jnp.repeat(jnp.exp(heights), dims[position] // blocks).reshape((-1,) + (1,) * (len(dims) - 1 - position))
    return factor_of


def noise(rng, dims, deviation, limit, cuts=(), held_as=jnp.bfloat16):
    array = deviation * jax.random.normal(rng, dims, jnp.float32)
    if cuts:
        array = array * steps_of(rng, dims, cuts, -0.22, 0.18)
    return jnp.clip(array, -limit, limit).astype(held_as)


def setup_inputs(seed: int = 0) -> dict:
    splits = jax.random.split(jax.random.key(seed), 8)
    state = noise(splits[0], (PATTERNS, Q), 1.0, 6.0, ((0, 64), (1, 2)), jnp.float32)
    queue_blocks = noise(splits[1], (QB, 3, BS, BS), (3 * BS) ** -0.5, 0.21875, ((0, 2),), jnp.float32)
    queue_rows = draw_queue_rows(jax.random.fold_in(splits[7], 71), 0)
    kill_blocks = noise(splits[3], (QB, 3, BS, BS), (3 * BS) ** -0.5, 0.21875, ((0, 2),), jnp.float32)
    kill_rows = draw_kill_rows(jax.random.fold_in(splits[7], 71), 0)
    rate_index = plant(jax.random.randint(splits[5], (RACKS,), 0, NRATES), jax.random.fold_in(splits[5], 1), 0, NRATES - 1).astype(jnp.int32)
    rate_table = jnp.clip(jnp.exp(jax.random.uniform(splits[6], (NRATES, 2), jnp.float32, math.log(0.1), math.log(2.0))), 0.1, 2.0)
    return {"state": state, "queue_blocks": queue_blocks, "queue_rows": queue_rows, "kill_blocks": kill_blocks, "kill_rows": kill_rows, "rate_index": rate_index, "rate_table": rate_table}


def apply_blocks(full, blocks, rows):
    pieces = full.reshape(PATTERNS, QB, BS)

    def one_column(item):
        weights, picks = item
        chosen = jnp.take(pieces, picks, axis=1).reshape(PATTERNS, 3 * BS)
        return jnp.dot(chosen, weights.reshape(3 * BS, BS), precision=lax.Precision.HIGHEST, preferred_element_type=jnp.float32)

    columns = lax.map(one_column, (blocks, rows))
    return jnp.transpose(columns, (1, 0, 2)).reshape(PATTERNS, Q)


def bit_terms(current, killed, fail, repair, first, count):
    total = jnp.zeros_like(current)
    rows = current.shape[0]
    for bit in range(count):
        shape = (rows // 2 ** (bit + 1), 2, 2 ** bit) + current.shape[1:]
        upper = current.reshape(shape)
        lower = killed.reshape(shape)
        term = jnp.stack((repair[first + bit] * upper[:, 1], fail[first + bit] * lower[:, 0]), axis=1)
        total = total + term.reshape(current.shape)
    return total


def reference(state, queue_blocks, queue_rows, kill_blocks, kill_rows, rate_index, rate_table):
    fail = rate_table[rate_index, 0]
    repair = rate_table[rate_index, 1]
    scale_sum = 1.0 + jnp.sum(fail + repair)
    pattern = lax.broadcasted_iota(jnp.int32, (PATTERNS, 1), 0)
    leaving = jnp.zeros((PATTERNS, 1), jnp.float32)
    for rack_bit in range(RACKS):
        flag = (pattern // (2 ** rack_bit)) % 2
        leaving = leaving + jnp.where(flag == 1, repair[rack_bit], fail[rack_bit])
    current = state
    for step in range(STEPS):
        queue_part = apply_blocks(current, queue_blocks, queue_rows)
        killed = apply_blocks(current, kill_blocks, kill_rows)
        rack_part = bit_terms(current, killed, fail, repair, 0, RACKS)
        current = current + (queue_part + rack_part - leaving * current) / scale_sum
    return current
```

```python
import functools

import jax
import jax.numpy as jnp
from jax import lax
from jax.experimental import pallas as pl
from jax.experimental.pallas import tpu as pltpu
from jax.sharding import PartitionSpec as P

STEPS = 2
RACKS = 12
LOW = 6
CH = 2
R = 32
NB = 8
BS = 256
PIECES = 4
PB = NB // PIECES
SLOTS = 4
KINDS = 8
AG, YA, ZA, YB, ZB, CO, XF, XH = range(KINDS)
MESH = pl.DeviceIdType.MESH
F32 = jnp.float32
BF16 = jnp.bfloat16


def kernel(
    st, qw, kw, qrows, krows, rindex, rtable, out,
    vw, vhl, kb, qb, rya, rza, sy, sz, ryb, rzb, rco, rxf, rxh, ob,
    wst, whi, wlo, coef, rowc, diag,
    ssem, rsem, wsem, lsem, osem,
):
    rack = lax.axis_index("rack")
    me_q = lax.axis_index("queue")
    co = rack % 2
    xh = (rack // 2) % 2
    z0 = (rack // 4) % 2
    z1 = (rack // 8) % 2
    y0 = (rack // 16) % 2
    y1 = (rack // 32) % 2
    oq = 1 - me_q
    d_x1 = (rack, oq)
    d_x3 = (rack + 2 - 4 * xh, oq)
    d_co = (rack + 1 - 2 * co, me_q)
    d_z1 = (rack + 4 - 8 * z0, me_q)
    d_z3 = (rack + 4 - 8 * z0 + 8 - 16 * z1, me_q)
    d_y1 = (rack + 16 - 32 * y0, me_q)
    d_y3 = (rack + 16 - 32 * y0 + 32 - 64 * y1, me_q)
    own = me_q * NB
    other = oq * NB

    def load(ch, b):
        return pltpu.make_async_copy(
            st.at[pl.ds(ch * R, R), pl.ds(b * BS, BS)], vw.at[0, ch, own + b], lsem.at[ch, b]
        )

    for ch in range(CH):
        for b in range(NB):
            load(ch, b).start()

    def weight(u):
        src = qw if u % 2 == 0 else kw
        return pltpu.make_async_copy(src.at[u // 2], wst.at[u % SLOTS], wsem.at[u % SLOTS])

    for u in range(SLOTS):
        weight(u).start()

    barrier = pltpu.get_barrier_semaphore()
    partners = (d_x1, d_x3, d_co, d_z1, d_z3, d_y1, d_y3)
    for d in partners:
        pl.semaphore_signal(barrier, inc=1, device_id=d, device_id_type=MESH)

    fail = [rtable[0, rindex[r]] for r in range(RACKS)]
    repair = [rtable[1, rindex[r]] for r in range(RACKS)]
    total = 1.0
    for r in range(RACKS):
        total = total + (fail[r] + repair[r])
    inv = 1.0 / jnp.full((8, BS), total, F32)
    for r in range(RACKS):
        coef[r] = fail[r] * inv
        coef[RACKS + r] = repair[r] * inv
    coef[24] = inv
    pick = lambda flag, a, b: jnp.where(flag == 1, a, b)
    coef[25] = pick(co, fail[6], repair[6]) * inv
    coef[26] = pick(xh, fail[7], repair[7]) * inv
    coef[27] = pick(y0, 0.0, fail[10]) * inv
    coef[28] = pick(y0, repair[10], 0.0) * inv
    coef[29] = pick(y1, fail[11], repair[11]) * inv
    coef[30] = pick(z0, 0.0, fail[8]) * inv
    coef[31] = pick(z0, repair[8], 0.0) * inv
    coef[32] = pick(z1, fail[9], repair[9]) * inv
    sub = lax.broadcasted_iota(jnp.int32, (8, BS), 0)
    for b in range(3):
        bit = (sub // 2**b) % 2
        rowc[b] = jnp.where(bit == 1, fail[b] * inv, 0.0)
        rowc[3 + b] = jnp.where(bit == 0, repair[b] * inv, 0.0)
    high = (
        pick(co, repair[6], fail[6]) + pick(xh, repair[7], fail[7])
        + pick(z0, repair[8], fail[8]) + pick(z1, repair[9], fail[9])
        + pick(y0, repair[10], fail[10]) + pick(y1, repair[11], fail[11])
    )
    for ch in range(CH):
        for i in range(R // 8):
            ex = high + (repair[5] if ch else fail[5])
            ex = ex + (repair[3] if i % 2 else fail[3]) + (repair[4] if i // 2 else fail[4])
            leave = jnp.full((8, BS), ex, F32)
            for b in range(3):
                leave = leave + jnp.where((sub // 2**b) % 2 == 1, repair[b], fail[b])
            diag[ch, i] = 1.0 - leave * inv

    def rdma(kind, s, ch, p, src, dst, dev):
        return pltpu.make_async_remote_copy(
            src_ref=src, dst_ref=dst, send_sem=ssem.at[kind, s, ch, p],
            recv_sem=rsem.at[kind, s, ch, p], device_id=dev, device_id_type=MESH,
        )

    def blocks(ref, s, ch, p):
        return ref.at[s, ch, pl.ds(p * PB, PB)]

    def mine(s, ch, p):
        return vw.at[s, ch, pl.ds(own + p * PB, PB)]

    def copy(kind, s, ch, p, src=None):
        if src is None:
            src = blocks(kb, s, ch, p)
        if kind == AG:
            return rdma(kind, s, ch, p, mine(s, ch, p), mine(s, ch, p), d_x1)
        dst, dev = {
            YA: (rya, d_y3), ZA: (rza, d_z3), YB: (ryb, d_y1), ZB: (rzb, d_z1), CO: (rco, d_co),
        }[kind]
        return rdma(kind, s, ch, p, src, blocks(dst, s, ch, p), dev)

    def relay(s, ch, p, src):
        return rdma(XF, s, ch, p, src, rxf.at[s, ch, pl.ds((p * PB) % (NB // 2), PB)],
                    d_x1 if p < PIECES // 2 else d_x3)

    def relayed(s, ch, p):
        return rxf.at[s, ch, pl.ds((p * PB) % (NB // 2), PB)]

    def final_x(s, ch, p, src, dev, sent=XH):
        return pltpu.make_async_remote_copy(
            src_ref=src, dst_ref=blocks(rxh, s, ch, p), send_sem=ssem.at[sent, s, ch, p],
            recv_sem=rsem.at[XH, s, ch, p], device_id=dev, device_id_type=MESH,
        )

    def send_c(s, ch, p):
        copy(AG, s, ch, p).start()

        @pl.when(y1 == 1)
        def _():
            copy(YA, s, ch, p, mine(s, ch, p)).start()

        @pl.when(z1 == 1)
        def _():
            copy(ZA, s, ch, p, mine(s, ch, p)).start()

        @pl.when(co == 1)
        def _():
            copy(CO, s, ch, p, mine(s, ch, p)).start()

    def send_k(s, ch, p):
        @pl.when(xh == 0)
        def _():
            relay(s, ch, p, blocks(kb, s, ch, p)).start()

        @pl.when(y1 == 0)
        def _():
            copy(YA, s, ch, p).start()

        @pl.when(z1 == 0)
        def _():
            copy(ZA, s, ch, p).start()

        @pl.when(co == 0)
        def _():
            copy(CO, s, ch, p).start()

    def split_block(s, ch, b):
        x = vw[s, ch, b]
        hi = x.astype(BF16)
        vhl[b, :R, :] = hi
        vhl[b, R:, :] = (x - hi.astype(F32)).astype(BF16)

    def recv_ag(s, ch):
        @pl.loop(0, NB)
        def _(b):
            split_block(s, ch, own + b)

        for p in range(PIECES):
            theirs = vw.at[s, ch, pl.ds(other + p * PB, PB)]
            rdma(AG, s, ch, p, theirs, theirs, d_x1).wait_recv()

            @pl.when(xh == 1)
            def _(p=p, theirs=theirs):
                final_x(s, ch, p, theirs, d_x3).start()

            @pl.loop(0, PB)
            def _(b, p=p):
                split_block(s, ch, other + p * PB + b)

    def product(rows, c, m):
        lhs = jnp.concatenate([vhl[rows[c, j]] for j in range(3)], axis=1)
        a = jnp.dot(lhs, whi[m, c], preferred_element_type=F32)
        b = jnp.dot(lhs[:R], wlo[m, c], preferred_element_type=F32)
        return a[:R] + a[R:] + b

    def mm(s, ch, p):
        @pl.loop(p * PB, (p + 1) * PB)
        def _(c):
            kb[s, ch, c] = product(krows, c, 1)
            qb[ch, c] = product(qrows, c, 0)

        send_k(s, ch, p)

    def forward(s, ch, p):
        if p < PIECES // 2:
            @pl.when(xh == 0)
            def _():
                relay(s, ch, p, relayed(s, ch, p)).wait_recv()
                final_x(s, ch, p, relayed(s, ch, p), d_x3).start()
        else:
            @pl.when(xh == 1)
            def _():
                relay(s, ch, p, relayed(s, ch, p)).wait_recv()
                final_x(s, ch, p, relayed(s, ch, p), d_x1, XF).start()

    def sums(s, ch, p):
        forward(s, ch, p)
        for kind, recv, send, at, nxt in ((YA, rya, sy, 27, YB), (ZA, rza, sz, 30, ZB)):
            copy(kind, s, ch, p).wait_recv()

            @pl.loop(0, PB)
            def _(b, recv=recv, send=send, at=at):
                c = p * PB + b
                ca, cb, cc = coef[at], coef[at + 1], coef[at + 2]
                for i in range(R // 8):
                    rs = pl.ds(i * 8, 8)
                    send[s, ch, c, rs, :] = (
                        ca * kb[s, ch, c, rs, :] + cb * vw[s, ch, own + c, rs, :] + cc * recv[s, ch, c, rs, :]
                    )

            copy(nxt, s, ch, p, blocks(send, s, ch, p)).start()

    def comb(s, ch, p):
        for kind in (CO, YB, ZB):
            copy(kind, s, ch, p).wait_recv()
        final_x(s, ch, p, blocks(rxh, s, ch, p), d_x3).wait_recv()

        @pl.loop(0, PB)
        def _(b):
            c = p * PB + b
            n = R // 8
            rs = [pl.ds(i * 8, 8) for i in range(n)]
            cur = [vw[s, ch, own + c, r, :] for r in rs]
            kil = [kb[s, ch, c, r, :] for r in rs]
            for i in range(n):
                acc = diag[ch, i] * cur[i] + coef[24] * qb[ch, c, rs[i], :]
                for t in range(3):
                    acc = acc + rowc[t] * pltpu.roll(kil[i], 2**t, 0)
                    acc = acc + rowc[3 + t] * pltpu.roll(cur[i], 8 - 2**t, 0)
                acc = acc + (coef[3] * kil[i - 1] if i % 2 else coef[15] * cur[i + 1])
                acc = acc + (coef[4] * kil[i - 2] if i // 2 else coef[16] * cur[i + 2])
                if ch == 0:
                    acc = acc + coef[17] * vw[s, 1, own + c, rs[i], :]
                else:
                    acc = acc + coef[5] * kb[s, 0, c, rs[i], :]
                acc = acc + coef[25] * rco[s, ch, c, rs[i], :]
                acc = acc + coef[26] * rxh[s, ch, c, rs[i], :]
                acc = acc + ryb[s, ch, c, rs[i], :] + rzb[s, ch, c, rs[i], :]
                if s + 1 < STEPS:
                    vw[s + 1, ch, own + c, rs[i], :] = acc
                else:
                    ob[ch, c, rs[i], :] = acc

        if s + 1 < STEPS:
            send_c(s + 1, ch, p)
        else:
            for b in range(PB):
                store(ch, p * PB + b).start()

    def store(ch, b):
        return pltpu.make_async_copy(
            ob.at[ch, b], out.at[pl.ds(ch * R, R), pl.ds(b * BS, BS)], osem.at[ch, b]
        )

    for b in range(NB):
        load(0, b).wait()
    pl.semaphore_wait(barrier, len(partners))
    for p in range(PIECES):
        send_c(0, 0, p)
    for b in range(NB):
        load(1, b).wait()
    for p in range(PIECES):
        send_c(0, 1, p)

    for u in range(2 * NB):
        weight(u).wait()

        @pl.loop(0, 24)
        def _(i, u=u):
            rs = pl.ds(pl.multiple_of(i * 32, 32), 32)
            x = wst[u % SLOTS, rs, :]
            hi = x.astype(BF16)
            whi[u % 2, u // 2, rs, :] = hi
            wlo[u % 2, u // 2, rs, :] = (x - hi.astype(F32)).astype(BF16)

        if u + SLOTS < 2 * NB:
            weight(u + SLOTS).start()

    every = range(PIECES)

    def products(s, ch):
        recv_ag(s, ch)
        for p in every:
            mm(s, ch, p)

    def all_of(f, s, ch):
        for p in every:
            f(s, ch, p)

    products(0, 0)
    all_of(sums, 0, 0)
    products(0, 1)
    all_of(comb, 0, 0)
    all_of(sums, 0, 1)
    all_of(comb, 0, 1)
    products(1, 0)
    all_of(sums, 1, 0)
    products(1, 1)
    all_of(comb, 1, 0)
    all_of(sums, 1, 1)
    all_of(comb, 1, 1)

    for s in range(STEPS):
        for ch in range(CH):
            for p in every:
                for kind in (AG, YA, ZA, YB, ZB, CO):
                    copy(kind, s, ch, p).wait_send()

                first = p < PIECES // 2
                for kind, sender in ((XF, 0 if first else None), (XH, 1 if not first else None)):
                    if sender is None:
                        final_x(s, ch, p, relayed(s, ch, p), d_x3, kind).wait_send()
                    else:
                        @pl.when(xh == sender)
                        def _(s=s, ch=ch, p=p, kind=kind):
                            final_x(s, ch, p, relayed(s, ch, p), d_x3, kind).wait_send()

    for ch in range(CH):
        for b in range(NB):
            store(ch, b).wait()


def local(state, queue_blocks, queue_rows, kill_blocks, kill_rows, rate_index, rate_table):
    buf = lambda *shape: pltpu.VMEM(shape, F32)
    full = (STEPS, CH, NB, R, BS)
    return pl.pallas_call(
        kernel,
        out_shape=jax.ShapeDtypeStruct(state.shape, F32),
        in_specs=[pl.BlockSpec(memory_space=pl.ANY)] * 3
        + [pl.BlockSpec(memory_space=pltpu.SMEM)] * 4,
        out_specs=pl.BlockSpec(memory_space=pl.ANY),
        scratch_shapes=[
            buf(STEPS, CH, 2 * NB, R, BS),
            pltpu.VMEM((2 * NB, 2 * R, BS), BF16),
            buf(*full),
            buf(CH, NB, R, BS),
            buf(*full), buf(*full),
            buf(*full), buf(*full),
            buf(*full), buf(*full),
            buf(*full),
            buf(STEPS, CH, NB // 2, R, BS),
            buf(*full),
            buf(CH, NB, R, BS),
            buf(SLOTS, 3 * BS, BS),
            pltpu.VMEM((2, NB, 3 * BS, BS), BF16),
            pltpu.VMEM((2, NB, 3 * BS, BS), BF16),
            buf(33, 8, BS), buf(6, 8, BS), buf(CH, R // 8, 8, BS),
            pltpu.SemaphoreType.DMA((KINDS, STEPS, CH, PIECES)),
            pltpu.SemaphoreType.DMA((KINDS, STEPS, CH, PIECES)),
            pltpu.SemaphoreType.DMA((SLOTS,)),
            pltpu.SemaphoreType.DMA((CH, NB)),
            pltpu.SemaphoreType.DMA((CH, NB)),
        ],
        compiler_params=pltpu.CompilerParams(
            collective_id=0, has_side_effects=True, vmem_limit_bytes=60 * 1024 * 1024
        ),
        name="chain",
    )(
        state,
        queue_blocks.reshape(NB, 3 * BS, BS),
        kill_blocks.reshape(NB, 3 * BS, BS),
        queue_rows, kill_rows, rate_index, rate_table.T,
    )


def solution(mesh):
    placed = (
        P("rack", "queue"),
        P("queue", None, None, None),
        P("queue", None),
        P("queue", None, None, None),
        P("queue", None),
        P(),
        P(),
    )
    return jax.shard_map(
        local, mesh=mesh, in_specs=placed, out_specs=P("rack", "queue"), check_vma=False
    )
```

```python
import functools

import jax
import jax.numpy as jnp
from jax import lax
from jax.experimental import pallas as pl
from jax.experimental.pallas import tpu as pltpu
from jax.sharding import PartitionSpec as P

STEPS = 2
RACKS = 12
LOW = 6
CH = 2
R = 32
NB = 8
BS = 256
PIECES = 4
PB = NB // PIECES
SLOTS = 2 * NB
KINDS = 8
AG, YA, ZA, YB, ZB, CO, XF, XH = range(KINDS)
MESH = pl.DeviceIdType.MESH
F32 = jnp.float32
BF16 = jnp.bfloat16


def kernel(
    st, qw, kw, qrows, krows, rindex, rtable, out,
    vw, vhl, kb, qb, rya, rza, sy, sz, ryb, rzb, rco, rxf, rxh, ob,
    wst, whi, wlo, coef, rowc, diag,
    ssem, rsem, wsem, lsem, osem,
):
    rack = lax.axis_index("rack")
    me_q = lax.axis_index("queue")
    co = rack % 2
    xh = (rack // 2) % 2
    z0 = (rack // 4) % 2
    z1 = (rack // 8) % 2
    y0 = (rack // 16) % 2
    y1 = (rack // 32) % 2
    oq = 1 - me_q
    d_x1 = (rack, oq)
    d_x3 = (rack + 2 - 4 * xh, oq)
    d_co = (rack + 1 - 2 * co, me_q)
    d_z1 = (rack + 4 - 8 * z0, me_q)
    d_z3 = (rack + 4 - 8 * z0 + 8 - 16 * z1, me_q)
    d_y1 = (rack + 16 - 32 * y0, me_q)
    d_y3 = (rack + 16 - 32 * y0 + 32 - 64 * y1, me_q)
    own = me_q * NB
    other = oq * NB

    def load(ch, b):
        return pltpu.make_async_copy(
            st.at[pl.ds(ch * R, R), pl.ds(b * BS, BS)], vw.at[0, ch, own + b], lsem.at[ch, b]
        )

    for ch in range(CH):
        for b in range(NB):
            load(ch, b).start()

    def weight(u):
        src = kw if u < NB else qw
        return pltpu.make_async_copy(src.at[u % NB], wst.at[u], wsem.at[u])

    for u in range(SLOTS):
        weight(u).start()

    barrier = pltpu.get_barrier_semaphore()
    partners = (d_x1, d_x3, d_co, d_z1, d_z3, d_y1, d_y3)
    for d in partners:
        pl.semaphore_signal(barrier, inc=1, device_id=d, device_id_type=MESH)

    fail = [rtable[0, rindex[r]] for r in range(RACKS)]
    repair = [rtable[1, rindex[r]] for r in range(RACKS)]
    total = 1.0
    for r in range(RACKS):
        total = total + (fail[r] + repair[r])
    inv = 1.0 / jnp.full((8, BS), total, F32)
    for r in range(RACKS):
        coef[r] = fail[r] * inv
        coef[RACKS + r] = repair[r] * inv
    coef[24] = inv
    pick = lambda flag, a, b: jnp.where(flag == 1, a, b)
    coef[25] = pick(co, fail[6], repair[6]) * inv
    coef[26] = pick(xh, fail[7], repair[7]) * inv
    coef[27] = pick(y0, 0.0, fail[10]) * inv
    coef[28] = pick(y0, repair[10], 0.0) * inv
    coef[29] = pick(y1, fail[11], repair[11]) * inv
    coef[30] = pick(z0, 0.0, fail[8]) * inv
    coef[31] = pick(z0, repair[8], 0.0) * inv
    coef[32] = pick(z1, fail[9], repair[9]) * inv
    sub = lax.broadcasted_iota(jnp.int32, (8, BS), 0)
    for b in range(3):
        bit = (sub // 2**b) % 2
        rowc[b] = jnp.where(bit == 1, fail[b] * inv, 0.0)
        rowc[3 + b] = jnp.where(bit == 0, repair[b] * inv, 0.0)
    high = (
        pick(co, repair[6], fail[6]) + pick(xh, repair[7], fail[7])
        + pick(z0, repair[8], fail[8]) + pick(z1, repair[9], fail[9])
        + pick(y0, repair[10], fail[10]) + pick(y1, repair[11], fail[11])
    )
    for ch in range(CH):
        for i in range(R // 8):
            ex = high + (repair[5] if ch else fail[5])
            ex = ex + (repair[3] if i % 2 else fail[3]) + (repair[4] if i // 2 else fail[4])
            leave = jnp.full((8, BS), ex, F32)
            for b in range(3):
                leave = leave + jnp.where((sub // 2**b) % 2 == 1, repair[b], fail[b])
            diag[ch, i] = 1.0 - leave * inv

    def rdma(kind, s, ch, p, src, dst, dev):
        return pltpu.make_async_remote_copy(
            src_ref=src, dst_ref=dst, send_sem=ssem.at[kind, s, ch, p],
            recv_sem=rsem.at[kind, s, ch, p], device_id=dev, device_id_type=MESH,
        )

    def blocks(ref, s, ch, p):
        return ref.at[s, ch, pl.ds(p * PB, PB)]

    def mine(s, ch, p):
        return vw.at[s, ch, pl.ds(own + p * PB, PB)]

    def copy(kind, s, ch, p, src=None):
        if src is None:
            src = blocks(kb, s, ch, p)
        if kind == AG:
            return rdma(kind, s, ch, p, mine(s, ch, p), mine(s, ch, p), d_x1)
        dst, dev = {
            YA: (rya, d_y3), ZA: (rza, d_z3), YB: (ryb, d_y1), ZB: (rzb, d_z1), CO: (rco, d_co),
        }[kind]
        return rdma(kind, s, ch, p, src, blocks(dst, s, ch, p), dev)

    def relay(s, ch, p, src):
        return rdma(XF, s, ch, p, src, rxf.at[s, ch, pl.ds((p * PB) % (NB // 2), PB)],
                    d_x1 if p < PIECES // 2 else d_x3)

    def relayed(s, ch, p):
        return rxf.at[s, ch, pl.ds((p * PB) % (NB // 2), PB)]

    def final_x(s, ch, p, src, dev, sent=XH):
        return pltpu.make_async_remote_copy(
            src_ref=src, dst_ref=blocks(rxh, s, ch, p), send_sem=ssem.at[sent, s, ch, p],
            recv_sem=rsem.at[XH, s, ch, p], device_id=dev, device_id_type=MESH,
        )

    def send_c(s, ch, p):
        copy(AG, s, ch, p).start()

        @pl.when(y1 == 1)
        def _():
            copy(YA, s, ch, p, mine(s, ch, p)).start()

        @pl.when(z1 == 1)
        def _():
            copy(ZA, s, ch, p, mine(s, ch, p)).start()

        @pl.when(co == 1)
        def _():
            copy(CO, s, ch, p, mine(s, ch, p)).start()

    def send_k(s, ch, p):
        @pl.when(xh == 0)
        def _():
            relay(s, ch, p, blocks(kb, s, ch, p)).start()

        @pl.when(y1 == 0)
        def _():
            copy(YA, s, ch, p).start()

        @pl.when(z1 == 0)
        def _():
            copy(ZA, s, ch, p).start()

        @pl.when(co == 0)
        def _():
            copy(CO, s, ch, p).start()

    def split_block(s, ch, b):
        x = vw[s, ch, b]
        hi = x.astype(BF16)
        vhl[b, :R, :] = hi
        vhl[b, R:, :] = (x - hi.astype(F32)).astype(BF16)

    def recv_ag(s, ch):
        @pl.loop(0, NB)
        def _(b):
            split_block(s, ch, own + b)

        for p in range(PIECES):
            theirs = vw.at[s, ch, pl.ds(other + p * PB, PB)]
            rdma(AG, s, ch, p, theirs, theirs, d_x1).wait_recv()

            @pl.when(xh == 1)
            def _(p=p, theirs=theirs):
                final_x(s, ch, p, theirs, d_x3).start()

            @pl.loop(0, PB)
            def _(b, p=p):
                split_block(s, ch, other + p * PB + b)

    def product(rows, c, m):
        lhs = jnp.concatenate([vhl[rows[j, c]] for j in range(3)], axis=1)
        a = jnp.dot(lhs, whi[m, c], preferred_element_type=F32)
        b = jnp.dot(lhs[:R], wlo[m, c], preferred_element_type=F32)
        return a[:R] + a[R:] + b

    def kill(s, ch, p):
        @pl.loop(p * PB, (p + 1) * PB)
        def _(c):
            kb[s, ch, c] = product(krows, c, 1)

        send_k(s, ch, p)

    def queue(ch):
        @pl.loop(0, NB)
        def _(c):
            qb[ch, c] = product(qrows, c, 0)

    def forward(s, ch, p):
        if p < PIECES // 2:
            @pl.when(xh == 0)
            def _():
                relay(s, ch, p, relayed(s, ch, p)).wait_recv()
                final_x(s, ch, p, relayed(s, ch, p), d_x3).start()
        else:
            @pl.when(xh == 1)
            def _():
                relay(s, ch, p, relayed(s, ch, p)).wait_recv()
                final_x(s, ch, p, relayed(s, ch, p), d_x1, XF).start()

    def sums(s, ch, p):
        for kind, recv, send, at, nxt in ((YA, rya, sy, 27, YB), (ZA, rza, sz, 30, ZB)):
            copy(kind, s, ch, p).wait_recv()

            @pl.loop(0, PB)
            def _(b, recv=recv, send=send, at=at):
                c = p * PB + b
                ca, cb, cc = coef[at], coef[at + 1], coef[at + 2]
                for i in range(R // 8):
                    rs = pl.ds(i * 8, 8)
                    send[s, ch, c, rs, :] = (
                        ca * kb[s, ch, c, rs, :] + cb * vw[s, ch, own + c, rs, :] + cc * recv[s, ch, c, rs, :]
                    )

            copy(nxt, s, ch, p, blocks(send, s, ch, p)).start()

    def comb(s, ch, p):
        for kind in (CO, YB, ZB):
            copy(kind, s, ch, p).wait_recv()
        final_x(s, ch, p, blocks(rxh, s, ch, p), d_x3).wait_recv()

        @pl.loop(0, PB)
        def _(b):
            c = p * PB + b
            n = R // 8
            rs = [pl.ds(i * 8, 8) for i in range(n)]
            cur = [vw[s, ch, own + c, r, :] for r in rs]
            kil = [kb[s, ch, c, r, :] for r in rs]
            for i in range(n):
                acc = diag[ch, i] * cur[i] + coef[24] * qb[ch, c, rs[i], :]
                for t in range(3):
                    acc = acc + rowc[t] * pltpu.roll(kil[i], 2**t, 0)
                    acc = acc + rowc[3 + t] * pltpu.roll(cur[i], 8 - 2**t, 0)
                acc = acc + (coef[3] * kil[i - 1] if i % 2 else coef[15] * cur[i + 1])
                acc = acc + (coef[4] * kil[i - 2] if i // 2 else coef[16] * cur[i + 2])
                if ch == 0:
                    acc = acc + coef[17] * vw[s, 1, own + c, rs[i], :]
                else:
                    acc = acc + coef[5] * kb[s, 0, c, rs[i], :]
                acc = acc + coef[25] * rco[s, ch, c, rs[i], :]
                acc = acc + coef[26] * rxh[s, ch, c, rs[i], :]
                acc = acc + ryb[s, ch, c, rs[i], :] + rzb[s, ch, c, rs[i], :]
                if s + 1 < STEPS:
                    vw[s + 1, ch, own + c, rs[i], :] = acc
                else:
                    ob[ch, c, rs[i], :] = acc

        if s + 1 < STEPS:
            send_c(s + 1, ch, p)
        else:
            for b in range(PB):
                store(ch, p * PB + b).start()

    def store(ch, b):
        return pltpu.make_async_copy(
            ob.at[ch, b], out.at[pl.ds(ch * R, R), pl.ds(b * BS, BS)], osem.at[ch, b]
        )

    for b in range(NB):
        load(0, b).wait()
    pl.semaphore_wait(barrier, len(partners))
    for p in range(PIECES):
        send_c(0, 0, p)
    for b in range(NB):
        load(1, b).wait()
    for p in range(PIECES):
        send_c(0, 1, p)

    def weights(m):
        for c in range(NB):
            u = (1 - m) * NB + c
            weight(u).wait()

            @pl.loop(0, 24)
            def _(i, u=u, c=c):
                rs = pl.ds(pl.multiple_of(i * 32, 32), 32)
                x = wst[u, rs, :]
                hi = x.astype(BF16)
                whi[m, c, rs, :] = hi
                wlo[m, c, rs, :] = (x - hi.astype(F32)).astype(BF16)

    every = range(PIECES)
    early, late = every[: PIECES // 2], every[PIECES // 2 :]

    def all_of(f, s, ch, pieces=every):
        for p in pieces:
            f(s, ch, p)

    weights(1)
    for s in range(STEPS):
        recv_ag(s, 0)
        all_of(kill, s, 0)
        if s == 0:
            weights(0)
        queue(0)
        all_of(sums, s, 0, early)
        all_of(forward, s, 0, late)
        recv_ag(s, 1)
        all_of(kill, s, 1)
        all_of(sums, s, 0, late)
        all_of(forward, s, 0, early)
        queue(1)
        for p in every:
            comb(s, 0, p)
            sums(s, 1, p)
        all_of(forward, s, 1, late)
        all_of(forward, s, 1, early)
        all_of(comb, s, 1)

    for s in range(STEPS):
        for ch in range(CH):
            for p in every:
                for kind in (AG, YA, ZA, YB, ZB, CO):
                    copy(kind, s, ch, p).wait_send()

                first = p < PIECES // 2
                for kind, sender in ((XF, 0 if first else None), (XH, 1 if not first else None)):
                    if sender is None:
                        final_x(s, ch, p, relayed(s, ch, p), d_x3, kind).wait_send()
                    else:
                        @pl.when(xh == sender)
                        def _(s=s, ch=ch, p=p, kind=kind):
                            final_x(s, ch, p, relayed(s, ch, p), d_x3, kind).wait_send()

    for ch in range(CH):
        for b in range(NB):
            store(ch, b).wait()


def local(state, queue_blocks, queue_rows, kill_blocks, kill_rows, rate_index, rate_table):
    buf = lambda *shape: pltpu.VMEM(shape, F32)
    full = (STEPS, CH, NB, R, BS)
    return pl.pallas_call(
        kernel,
        out_shape=jax.ShapeDtypeStruct(state.shape, F32),
        in_specs=[pl.BlockSpec(memory_space=pl.ANY)] * 3
        + [pl.BlockSpec(memory_space=pltpu.SMEM)] * 4,
        out_specs=pl.BlockSpec(memory_space=pl.ANY),
        scratch_shapes=[
            buf(STEPS, CH, 2 * NB, R, BS),
            pltpu.VMEM((2 * NB, 2 * R, BS), BF16),
            buf(*full),
            buf(CH, NB, R, BS),
            buf(*full), buf(*full),
            buf(*full), buf(*full),
            buf(*full), buf(*full),
            buf(*full),
            buf(STEPS, CH, NB // 2, R, BS),
            buf(*full),
            buf(CH, NB, R, BS),
            buf(SLOTS, 3 * BS, BS),
            pltpu.VMEM((2, NB, 3 * BS, BS), BF16),
            pltpu.VMEM((2, NB, 3 * BS, BS), BF16),
            buf(33, 8, BS), buf(6, 8, BS), buf(CH, R // 8, 8, BS),
            pltpu.SemaphoreType.DMA((KINDS, STEPS, CH, PIECES)),
            pltpu.SemaphoreType.DMA((KINDS, STEPS, CH, PIECES)),
            pltpu.SemaphoreType.DMA((SLOTS,)),
            pltpu.SemaphoreType.DMA((CH, NB)),
            pltpu.SemaphoreType.DMA((CH, NB)),
        ],
        compiler_params=pltpu.CompilerParams(
            collective_id=0, has_side_effects=True, vmem_limit_bytes=60 * 1024 * 1024
        ),
        name="chain",
    )(
        state,
        queue_blocks.reshape(NB, 3 * BS, BS),
        kill_blocks.reshape(NB, 3 * BS, BS),
        queue_rows.T, kill_rows.T, rate_index, rate_table.T,
    )


def solution(mesh):
    placed = (
        P("rack", "queue"),
        P("queue", None, None, None),
        P("queue", None),
        P("queue", None, None, None),
        P("queue", None),
        P(),
        P(),
    )
    return jax.shard_map(
        local, mesh=mesh, in_specs=placed, out_specs=P("rack", "queue"), check_vma=False
    )
```

```python
import functools

import jax
import jax.numpy as jnp
from jax import lax
from jax.experimental import pallas as pl
from jax.experimental.pallas import tpu as pltpu
from jax.sharding import PartitionSpec as P

STEPS = 2
RACKS = 12
LOW = 6
CH = 2
R = 32
NB = 8
BS = 256
PIECES = 4
PB = NB // PIECES
SLOTS = 2 * NB
KINDS = 8
AG, YA, ZA, YB, ZB, CO, XF, XH = range(KINDS)
MESH = pl.DeviceIdType.MESH
F32 = jnp.float32
BF16 = jnp.bfloat16


def kernel(
    st, qw, kw, qrows, krows, rindex, rtable, out,
    vw, vhl, kb, qb, rya, rza, sy, sz, ryb, rzb, rco, rxf, rxh, ob,
    wst, whi, wlo, coef, rowc, diag,
    ssem, rsem, wsem, lsem, osem,
):
    rack = lax.axis_index("rack")
    me_q = lax.axis_index("queue")
    co = rack % 2
    xh = (rack // 2) % 2
    z0 = (rack // 4) % 2
    z1 = (rack // 8) % 2
    y0 = (rack // 16) % 2
    y1 = (rack // 32) % 2
    oq = 1 - me_q
    d_x1 = (rack, oq)
    d_x3 = (rack + 2 - 4 * xh, oq)
    d_co = (rack + 1 - 2 * co, me_q)
    d_z1 = (rack + 4 - 8 * z0, me_q)
    d_z3 = (rack + 4 - 8 * z0 + 8 - 16 * z1, me_q)
    d_y1 = (rack + 16 - 32 * y0, me_q)
    d_y3 = (rack + 16 - 32 * y0 + 32 - 64 * y1, me_q)
    own = me_q * NB
    other = oq * NB

    def load(ch, b):
        return pltpu.make_async_copy(
            st.at[pl.ds(ch * R, R), pl.ds(b * BS, BS)], vw.at[0, ch, own + b], lsem.at[ch, b]
        )

    for ch in range(CH):
        for b in range(NB):
            load(ch, b).start()

    def weight(u):
        src = kw if u < NB else qw
        return pltpu.make_async_copy(src.at[u % NB], wst.at[u], wsem.at[u])

    for u in range(SLOTS):
        weight(u).start()

    barrier = pltpu.get_barrier_semaphore()
    partners = (d_x1, d_x3, d_co, d_z1, d_z3, d_y1, d_y3)
    for d in partners:
        pl.semaphore_signal(barrier, inc=1, device_id=d, device_id_type=MESH)

    fail = [rtable[0, rindex[r]] for r in range(RACKS)]
    repair = [rtable[1, rindex[r]] for r in range(RACKS)]
    total = 1.0
    for r in range(RACKS):
        total = total + (fail[r] + repair[r])
    inv = 1.0 / jnp.full((8, BS), total, F32)
    for r in range(RACKS):
        coef[r] = fail[r] * inv
        coef[RACKS + r] = repair[r] * inv
    coef[24] = inv
    pick = lambda flag, a, b: jnp.where(flag == 1, a, b)
    coef[25] = pick(co, fail[6], repair[6]) * inv
    coef[26] = pick(xh, fail[7], repair[7]) * inv
    coef[27] = pick(y0, 0.0, fail[10]) * inv
    coef[28] = pick(y0, repair[10], 0.0) * inv
    coef[29] = pick(y1, fail[11], repair[11]) * inv
    coef[30] = pick(z0, 0.0, fail[8]) * inv
    coef[31] = pick(z0, repair[8], 0.0) * inv
    coef[32] = pick(z1, fail[9], repair[9]) * inv
    sub = lax.broadcasted_iota(jnp.int32, (8, BS), 0)
    for b in range(3):
        bit = (sub // 2**b) % 2
        rowc[b] = jnp.where(bit == 1, fail[b] * inv, 0.0)
        rowc[3 + b] = jnp.where(bit == 0, repair[b] * inv, 0.0)
    high = (
        pick(co, repair[6], fail[6]) + pick(xh, repair[7], fail[7])
        + pick(z0, repair[8], fail[8]) + pick(z1, repair[9], fail[9])
        + pick(y0, repair[10], fail[10]) + pick(y1, repair[11], fail[11])
    )
    for ch in range(CH):
        for i in range(R // 8):
            ex = high + (repair[5] if ch else fail[5])
            ex = ex + (repair[3] if i % 2 else fail[3]) + (repair[4] if i // 2 else fail[4])
            leave = jnp.full((8, BS), ex, F32)
            for b in range(3):
                leave = leave + jnp.where((sub // 2**b) % 2 == 1, repair[b], fail[b])
            diag[ch, i] = 1.0 - leave * inv

    def rdma(kind, s, ch, p, src, dst, dev):
        return pltpu.make_async_remote_copy(
            src_ref=src, dst_ref=dst, send_sem=ssem.at[kind, s, ch, p],
            recv_sem=rsem.at[kind, s, ch, p], device_id=dev, device_id_type=MESH,
        )

    def blocks(ref, s, ch, p):
        return ref.at[s, ch, pl.ds(p * PB, PB)]

    def mine(s, ch, p):
        return vw.at[s, ch, pl.ds(own + p * PB, PB)]

    def copy(kind, s, ch, p, src=None):
        if src is None:
            src = blocks(kb, s, ch, p)
        if kind == AG:
            return rdma(kind, s, ch, p, mine(s, ch, p), mine(s, ch, p), d_x1)
        dst, dev = {
            YA: (rya, d_y3), ZA: (rza, d_z3), YB: (ryb, d_y1), ZB: (rzb, d_z1), CO: (rco, d_co),
        }[kind]
        return rdma(kind, s, ch, p, src, blocks(dst, s, ch, p), dev)

    def relay(s, ch, p, src):
        return rdma(XF, s, ch, p, src, rxf.at[s, ch, pl.ds((p * PB) % (NB // 2), PB)],
                    d_x1 if p < PIECES // 2 else d_x3)

    def relayed(s, ch, p):
        return rxf.at[s, ch, pl.ds((p * PB) % (NB // 2), PB)]

    def final_x(s, ch, p, src, dev, sent=XH):
        return pltpu.make_async_remote_copy(
            src_ref=src, dst_ref=blocks(rxh, s, ch, p), send_sem=ssem.at[sent, s, ch, p],
            recv_sem=rsem.at[XH, s, ch, p], device_id=dev, device_id_type=MESH,
        )

    def send_c(s, ch, p):
        copy(AG, s, ch, p).start()

        @pl.when(y1 == 1)
        def _():
            copy(YA, s, ch, p, mine(s, ch, p)).start()

        @pl.when(z1 == 1)
        def _():
            copy(ZA, s, ch, p, mine(s, ch, p)).start()

        @pl.when(co == 1)
        def _():
            copy(CO, s, ch, p, mine(s, ch, p)).start()

    def send_k(s, ch, p):
        @pl.when(xh == 0)
        def _():
            relay(s, ch, p, blocks(kb, s, ch, p)).start()

        @pl.when(y1 == 0)
        def _():
            copy(YA, s, ch, p).start()

        @pl.when(z1 == 0)
        def _():
            copy(ZA, s, ch, p).start()

        @pl.when(co == 0)
        def _():
            copy(CO, s, ch, p).start()

    def split_block(s, ch, b):
        x = vw[s, ch, b]
        hi = x.astype(BF16)
        vhl[b, pl.ds(ch * R, R), :] = hi
        vhl[b, pl.ds((CH + ch) * R, R), :] = (x - hi.astype(F32)).astype(BF16)

    def recv_ag(s, ch):
        @pl.loop(0, NB)
        def _(b):
            split_block(s, ch, own + b)

        for p in range(PIECES):
            theirs = vw.at[s, ch, pl.ds(other + p * PB, PB)]
            rdma(AG, s, ch, p, theirs, theirs, d_x1).wait_recv()

            @pl.when(xh == 1)
            def _(p=p, theirs=theirs):
                final_x(s, ch, p, theirs, d_x3).start()

            @pl.loop(0, PB)
            def _(b, p=p):
                split_block(s, ch, other + p * PB + b)

    def product(lhs, m, c):
        n = lhs.shape[0] // 2
        a = jnp.dot(lhs, whi[m, c], preferred_element_type=F32)
        b = jnp.dot(lhs[:n], wlo[m, c], preferred_element_type=F32)
        return a[:n] + a[n:] + b

    def kill(s, ch, p):
        @pl.loop(p * PB, (p + 1) * PB)
        def _(c):
            part = lambda at: jnp.concatenate(
                [vhl[krows[j, c], pl.ds(at * R, R), :] for j in range(3)], axis=1
            )
            kb[s, ch, c] = product(jnp.concatenate([part(ch), part(CH + ch)], axis=0), 1, c)

        send_k(s, ch, p)

    def queue():
        @pl.loop(0, NB)
        def _(c):
            both = product(jnp.concatenate([vhl[qrows[j, c]] for j in range(3)], axis=1), 0, c)
            for ch in range(CH):
                qb[ch, c] = both[ch * R : (ch + 1) * R]

    def forward(s, ch, p):
        if p < PIECES // 2:
            @pl.when(xh == 0)
            def _():
                relay(s, ch, p, relayed(s, ch, p)).wait_recv()
                final_x(s, ch, p, relayed(s, ch, p), d_x3).start()
        else:
            @pl.when(xh == 1)
            def _():
                relay(s, ch, p, relayed(s, ch, p)).wait_recv()
                final_x(s, ch, p, relayed(s, ch, p), d_x1, XF).start()

    def sums(s, ch, p):
        for kind, recv, send, at, nxt in ((YA, rya, sy, 27, YB), (ZA, rza, sz, 30, ZB)):
            copy(kind, s, ch, p).wait_recv()

            @pl.loop(0, PB)
            def _(b, recv=recv, send=send, at=at):
                c = p * PB + b
                ca, cb, cc = coef[at], coef[at + 1], coef[at + 2]
                for i in range(R // 8):
                    rs = pl.ds(i * 8, 8)
                    send[s, ch, c, rs, :] = (
                        ca * kb[s, ch, c, rs, :] + cb * vw[s, ch, own + c, rs, :] + cc * recv[s, ch, c, rs, :]
                    )

            copy(nxt, s, ch, p, blocks(send, s, ch, p)).start()

    def comb(s, ch, p):
        for kind in (CO, YB, ZB):
            copy(kind, s, ch, p).wait_recv()
        final_x(s, ch, p, blocks(rxh, s, ch, p), d_x3).wait_recv()

        @pl.loop(0, PB)
        def _(b):
            c = p * PB + b
            n = R // 8
            rs = [pl.ds(i * 8, 8) for i in range(n)]
            cur = [vw[s, ch, own + c, r, :] for r in rs]
            kil = [kb[s, ch, c, r, :] for r in rs]
            for i in range(n):
                acc = diag[ch, i] * cur[i] + coef[24] * qb[ch, c, rs[i], :]
                for t in range(3):
                    acc = acc + rowc[t] * pltpu.roll(kil[i], 2**t, 0)
                    acc = acc + rowc[3 + t] * pltpu.roll(cur[i], 8 - 2**t, 0)
                acc = acc + (coef[3] * kil[i - 1] if i % 2 else coef[15] * cur[i + 1])
                acc = acc + (coef[4] * kil[i - 2] if i // 2 else coef[16] * cur[i + 2])
                if ch == 0:
                    acc = acc + coef[17] * vw[s, 1, own + c, rs[i], :]
                else:
                    acc = acc + coef[5] * kb[s, 0, c, rs[i], :]
                acc = acc + coef[25] * rco[s, ch, c, rs[i], :]
                acc = acc + coef[26] * rxh[s, ch, c, rs[i], :]
                acc = acc + ryb[s, ch, c, rs[i], :] + rzb[s, ch, c, rs[i], :]
                if s + 1 < STEPS:
                    vw[s + 1, ch, own + c, rs[i], :] = acc
                else:
                    ob[ch, c, rs[i], :] = acc

        if s + 1 < STEPS:
            send_c(s + 1, ch, p)
        else:
            for b in range(PB):
                store(ch, p * PB + b).start()

    def store(ch, b):
        return pltpu.make_async_copy(
            ob.at[ch, b], out.at[pl.ds(ch * R, R), pl.ds(b * BS, BS)], osem.at[ch, b]
        )

    for b in range(NB):
        load(0, b).wait()
    pl.semaphore_wait(barrier, len(partners))
    for p in range(PIECES):
        send_c(0, 0, p)
    for b in range(NB):
        load(1, b).wait()
    for p in range(PIECES):
        send_c(0, 1, p)

    def weights(m):
        for c in range(NB):
            u = (1 - m) * NB + c
            weight(u).wait()

            @pl.loop(0, 24)
            def _(i, u=u, c=c):
                rs = pl.ds(pl.multiple_of(i * 32, 32), 32)
                x = wst[u, rs, :]
                hi = x.astype(BF16)
                whi[m, c, rs, :] = hi
                wlo[m, c, rs, :] = (x - hi.astype(F32)).astype(BF16)

    every = range(PIECES)
    early, late = every[: PIECES // 2], every[PIECES // 2 :]

    def all_of(f, s, ch, pieces=every):
        for p in pieces:
            f(s, ch, p)

    weights(1)
    weights(0)
    for s in range(STEPS):
        recv_ag(s, 0)
        all_of(kill, s, 0)
        all_of(sums, s, 0, early)
        all_of(forward, s, 0, late)
        recv_ag(s, 1)
        all_of(kill, s, 1)
        all_of(sums, s, 0, late)
        all_of(forward, s, 0, early)
        queue()
        all_of(forward, s, 1, late)
        for p in every:
            comb(s, 0, p)
            if p >= 2:
                sums(s, 1, p - 2)
        all_of(sums, s, 1, late)
        all_of(forward, s, 1, early)
        all_of(comb, s, 1)

    for s in range(STEPS):
        for ch in range(CH):
            for p in every:
                for kind in (AG, YA, ZA, YB, ZB, CO):
                    copy(kind, s, ch, p).wait_send()

                first = p < PIECES // 2
                for kind, sender in ((XF, 0 if first else None), (XH, 1 if not first else None)):
                    if sender is None:
                        final_x(s, ch, p, relayed(s, ch, p), d_x3, kind).wait_send()
                    else:
                        @pl.when(xh == sender)
                        def _(s=s, ch=ch, p=p, kind=kind):
                            final_x(s, ch, p, relayed(s, ch, p), d_x3, kind).wait_send()

    for ch in range(CH):
        for b in range(NB):
            store(ch, b).wait()


def local(state, queue_blocks, queue_rows, kill_blocks, kill_rows, rate_index, rate_table):
    buf = lambda *shape: pltpu.VMEM(shape, F32)
    full = (STEPS, CH, NB, R, BS)
    return pl.pallas_call(
        kernel,
        out_shape=jax.ShapeDtypeStruct(state.shape, F32),
        in_specs=[pl.BlockSpec(memory_space=pl.ANY)] * 3
        + [pl.BlockSpec(memory_space=pltpu.SMEM)] * 4,
        out_specs=pl.BlockSpec(memory_space=pl.ANY),
        scratch_shapes=[
            buf(STEPS, CH, 2 * NB, R, BS),
            pltpu.VMEM((2 * NB, 2 * CH * R, BS), BF16),
            buf(*full),
            buf(CH, NB, R, BS),
            buf(*full), buf(*full),
            buf(*full), buf(*full),
            buf(*full), buf(*full),
            buf(*full),
            buf(STEPS, CH, NB // 2, R, BS),
            buf(*full),
            buf(CH, NB, R, BS),
            buf(SLOTS, 3 * BS, BS),
            pltpu.VMEM((2, NB, 3 * BS, BS), BF16),
            pltpu.VMEM((2, NB, 3 * BS, BS), BF16),
            buf(33, 8, BS), buf(6, 8, BS), buf(CH, R // 8, 8, BS),
            pltpu.SemaphoreType.DMA((KINDS, STEPS, CH, PIECES)),
            pltpu.SemaphoreType.DMA((KINDS, STEPS, CH, PIECES)),
            pltpu.SemaphoreType.DMA((SLOTS,)),
            pltpu.SemaphoreType.DMA((CH, NB)),
            pltpu.SemaphoreType.DMA((CH, NB)),
        ],
        compiler_params=pltpu.CompilerParams(
            collective_id=0, has_side_effects=True, vmem_limit_bytes=60 * 1024 * 1024
        ),
        name="chain",
    )(
        state,
        queue_blocks.reshape(NB, 3 * BS, BS),
        kill_blocks.reshape(NB, 3 * BS, BS),
        queue_rows.T, kill_rows.T, rate_index, rate_table.T,
    )


def solution(mesh):
    placed = (
        P("rack", "queue"),
        P("queue", None, None, None),
        P("queue", None),
        P("queue", None, None, None),
        P("queue", None),
        P(),
        P(),
    )
    return jax.shard_map(
        local, mesh=mesh, in_specs=placed, out_specs=P("rack", "queue"), check_vma=False
    )
```

```python
import functools

import jax
import jax.numpy as jnp
from jax import lax
from jax.experimental import pallas as pl
from jax.experimental.pallas import tpu as pltpu
from jax.sharding import PartitionSpec as P

STEPS = 2
RACKS = 12
LOW = 6
CH = 2
R = 32
NB = 8
BS = 256
PIECES = 8
PB = NB // PIECES
SLOTS = 2 * NB
LAG = 4
KINDS = 8
AG, YA, ZA, YB, ZB, CO, XF, XH = range(KINDS)
MESH = pl.DeviceIdType.MESH
F32 = jnp.float32
BF16 = jnp.bfloat16


def kernel(
    st, qw, kw, qrows, krows, rindex, rtable, out,
    vw, vhl, kb, qb, rya, rza, sy, sz, ryb, rzb, rco, rxf, rxh, ob,
    wst, whi, wlo, coef, rowc, diag,
    ssem, rsem, wsem, lsem, osem,
):
    rack = lax.axis_index("rack")
    me_q = lax.axis_index("queue")
    co = rack % 2
    xh = (rack // 2) % 2
    z0 = (rack // 4) % 2
    z1 = (rack // 8) % 2
    y0 = (rack // 16) % 2
    y1 = (rack // 32) % 2
    oq = 1 - me_q
    d_x1 = (rack, oq)
    d_x3 = (rack + 2 - 4 * xh, oq)
    d_co = (rack + 1 - 2 * co, me_q)
    d_z1 = (rack + 4 - 8 * z0, me_q)
    d_z3 = (rack + 4 - 8 * z0 + 8 - 16 * z1, me_q)
    d_y1 = (rack + 16 - 32 * y0, me_q)
    d_y3 = (rack + 16 - 32 * y0 + 32 - 64 * y1, me_q)
    own = me_q * NB
    other = oq * NB

    def load(ch, b):
        return pltpu.make_async_copy(
            st.at[pl.ds(ch * R, R), pl.ds(b * BS, BS)], vw.at[0, ch, own + b], lsem.at[ch, b]
        )

    for ch in range(CH):
        for b in range(NB):
            load(ch, b).start()

    def weight(u):
        src = kw if u < NB else qw
        return pltpu.make_async_copy(src.at[u % NB], wst.at[u], wsem.at[u])

    for u in range(SLOTS):
        weight(u).start()

    barrier = pltpu.get_barrier_semaphore()
    partners = (d_x1, d_x3, d_co, d_z1, d_z3, d_y1, d_y3)
    for d in partners:
        pl.semaphore_signal(barrier, inc=1, device_id=d, device_id_type=MESH)

    fail = [rtable[0, rindex[r]] for r in range(RACKS)]
    repair = [rtable[1, rindex[r]] for r in range(RACKS)]
    total = 1.0
    for r in range(RACKS):
        total = total + (fail[r] + repair[r])
    inv = 1.0 / jnp.full((8, BS), total, F32)
    for r in range(RACKS):
        coef[r] = fail[r] * inv
        coef[RACKS + r] = repair[r] * inv
    coef[24] = inv
    pick = lambda flag, a, b: jnp.where(flag == 1, a, b)
    coef[25] = pick(co, fail[6], repair[6]) * inv
    coef[26] = pick(xh, fail[7], repair[7]) * inv
    coef[27] = pick(y0, 0.0, fail[10]) * inv
    coef[28] = pick(y0, repair[10], 0.0) * inv
    coef[29] = pick(y1, fail[11], repair[11]) * inv
    coef[30] = pick(z0, 0.0, fail[8]) * inv
    coef[31] = pick(z0, repair[8], 0.0) * inv
    coef[32] = pick(z1, fail[9], repair[9]) * inv
    sub = lax.broadcasted_iota(jnp.int32, (8, BS), 0)
    for b in range(3):
        bit = (sub // 2**b) % 2
        rowc[b] = jnp.where(bit == 1, fail[b] * inv, 0.0)
        rowc[3 + b] = jnp.where(bit == 0, repair[b] * inv, 0.0)
    high = (
        pick(co, repair[6], fail[6]) + pick(xh, repair[7], fail[7])
        + pick(z0, repair[8], fail[8]) + pick(z1, repair[9], fail[9])
        + pick(y0, repair[10], fail[10]) + pick(y1, repair[11], fail[11])
    )
    for ch in range(CH):
        for i in range(R // 8):
            ex = high + (repair[5] if ch else fail[5])
            ex = ex + (repair[3] if i % 2 else fail[3]) + (repair[4] if i // 2 else fail[4])
            leave = jnp.full((8, BS), ex, F32)
            for b in range(3):
                leave = leave + jnp.where((sub // 2**b) % 2 == 1, repair[b], fail[b])
            diag[ch, i] = 1.0 - leave * inv

    def rdma(kind, s, ch, p, src, dst, dev):
        return pltpu.make_async_remote_copy(
            src_ref=src, dst_ref=dst, send_sem=ssem.at[kind, s, ch, p],
            recv_sem=rsem.at[kind, s, ch, p], device_id=dev, device_id_type=MESH,
        )

    def blocks(ref, s, ch, p):
        return ref.at[s, ch, pl.ds(p * PB, PB)]

    def mine(s, ch, p):
        return vw.at[s, ch, pl.ds(own + p * PB, PB)]

    def copy(kind, s, ch, p, src=None):
        if src is None:
            src = blocks(kb, s, ch, p)
        if kind == AG:
            return rdma(kind, s, ch, p, mine(s, ch, p), mine(s, ch, p), d_x1)
        dst, dev = {
            YA: (rya, d_y3), ZA: (rza, d_z3), YB: (ryb, d_y1), ZB: (rzb, d_z1), CO: (rco, d_co),
        }[kind]
        return rdma(kind, s, ch, p, src, blocks(dst, s, ch, p), dev)

    def relay(s, ch, p, src):
        return rdma(XF, s, ch, p, src, rxf.at[s, ch, pl.ds((p * PB) % (NB // 2), PB)],
                    d_x1 if p < PIECES // 2 else d_x3)

    def relayed(s, ch, p):
        return rxf.at[s, ch, pl.ds((p * PB) % (NB // 2), PB)]

    def final_x(s, ch, p, src, dev, sent=XH):
        return pltpu.make_async_remote_copy(
            src_ref=src, dst_ref=blocks(rxh, s, ch, p), send_sem=ssem.at[sent, s, ch, p],
            recv_sem=rsem.at[XH, s, ch, p], device_id=dev, device_id_type=MESH,
        )

    def send_c(s, ch, p):
        copy(AG, s, ch, p).start()

        @pl.when(y1 == 1)
        def _():
            copy(YA, s, ch, p, mine(s, ch, p)).start()

        @pl.when(z1 == 1)
        def _():
            copy(ZA, s, ch, p, mine(s, ch, p)).start()

        @pl.when(co == 1)
        def _():
            copy(CO, s, ch, p, mine(s, ch, p)).start()

    def send_k(s, ch, p):
        @pl.when(xh == 0)
        def _():
            relay(s, ch, p, blocks(kb, s, ch, p)).start()

        @pl.when(y1 == 0)
        def _():
            copy(YA, s, ch, p).start()

        @pl.when(z1 == 0)
        def _():
            copy(ZA, s, ch, p).start()

        @pl.when(co == 0)
        def _():
            copy(CO, s, ch, p).start()

    def split_block(s, ch, b):
        x = vw[s, ch, b]
        hi = x.astype(BF16)
        vhl[b, pl.ds(ch * R, R), :] = hi
        vhl[b, pl.ds((CH + ch) * R, R), :] = (x - hi.astype(F32)).astype(BF16)

    def recv_ag(s, ch):
        @pl.loop(0, NB)
        def _(b):
            split_block(s, ch, own + b)

        for p in range(PIECES):
            theirs = vw.at[s, ch, pl.ds(other + p * PB, PB)]
            rdma(AG, s, ch, p, theirs, theirs, d_x1).wait_recv()

            @pl.when(xh == 1)
            def _(p=p, theirs=theirs):
                final_x(s, ch, p, theirs, d_x3).start()

            @pl.loop(0, PB)
            def _(b, p=p):
                split_block(s, ch, other + p * PB + b)

    def product(lhs, m, c):
        n = lhs.shape[0] // 2
        a = jnp.dot(lhs, whi[m, c], preferred_element_type=F32)
        b = jnp.dot(lhs[:n], wlo[m, c], preferred_element_type=F32)
        return a[:n] + a[n:] + b

    def kill(s, ch, p):
        @pl.loop(p * PB, (p + 1) * PB)
        def _(c):
            part = lambda at: jnp.concatenate(
                [vhl[krows[j, c], pl.ds(at * R, R), :] for j in range(3)], axis=1
            )
            kb[s, ch, c] = product(jnp.concatenate([part(ch), part(CH + ch)], axis=0), 1, c)

        send_k(s, ch, p)

    def queue():
        @pl.loop(0, NB)
        def _(c):
            both = product(jnp.concatenate([vhl[qrows[j, c]] for j in range(3)], axis=1), 0, c)
            for ch in range(CH):
                qb[ch, c] = both[ch * R : (ch + 1) * R]

    def forward(s, ch, p):
        if p < PIECES // 2:
            @pl.when(xh == 0)
            def _():
                relay(s, ch, p, relayed(s, ch, p)).wait_recv()
                final_x(s, ch, p, relayed(s, ch, p), d_x3).start()
        else:
            @pl.when(xh == 1)
            def _():
                relay(s, ch, p, relayed(s, ch, p)).wait_recv()
                final_x(s, ch, p, relayed(s, ch, p), d_x1, XF).start()

    def sums(s, ch, p):
        for kind, recv, send, at, nxt in ((YA, rya, sy, 27, YB), (ZA, rza, sz, 30, ZB)):
            copy(kind, s, ch, p).wait_recv()

            @pl.loop(0, PB)
            def _(b, recv=recv, send=send, at=at):
                c = p * PB + b
                ca, cb, cc = coef[at], coef[at + 1], coef[at + 2]
                for i in range(R // 8):
                    rs = pl.ds(i * 8, 8)
                    send[s, ch, c, rs, :] = (
                        ca * kb[s, ch, c, rs, :] + cb * vw[s, ch, own + c, rs, :] + cc * recv[s, ch, c, rs, :]
                    )

            copy(nxt, s, ch, p, blocks(send, s, ch, p)).start()

    def comb(s, ch, p):
        for kind in (CO, YB, ZB):
            copy(kind, s, ch, p).wait_recv()
        final_x(s, ch, p, blocks(rxh, s, ch, p), d_x3).wait_recv()

        @pl.loop(0, PB)
        def _(b):
            c = p * PB + b
            n = R // 8
            rs = [pl.ds(i * 8, 8) for i in range(n)]
            cur = [vw[s, ch, own + c, r, :] for r in rs]
            kil = [kb[s, ch, c, r, :] for r in rs]
            for i in range(n):
                acc = diag[ch, i] * cur[i] + coef[24] * qb[ch, c, rs[i], :]
                for t in range(3):
                    acc = acc + rowc[t] * pltpu.roll(kil[i], 2**t, 0)
                    acc = acc + rowc[3 + t] * pltpu.roll(cur[i], 8 - 2**t, 0)
                acc = acc + (coef[3] * kil[i - 1] if i % 2 else coef[15] * cur[i + 1])
                acc = acc + (coef[4] * kil[i - 2] if i // 2 else coef[16] * cur[i + 2])
                if ch == 0:
                    acc = acc + coef[17] * vw[s, 1, own + c, rs[i], :]
                else:
                    acc = acc + coef[5] * kb[s, 0, c, rs[i], :]
                acc = acc + coef[25] * rco[s, ch, c, rs[i], :]
                acc = acc + coef[26] * rxh[s, ch, c, rs[i], :]
                acc = acc + ryb[s, ch, c, rs[i], :] + rzb[s, ch, c, rs[i], :]
                if s + 1 < STEPS:
                    vw[s + 1, ch, own + c, rs[i], :] = acc
                else:
                    ob[ch, c, rs[i], :] = acc

        if s + 1 < STEPS:
            send_c(s + 1, ch, p)
        else:
            for b in range(PB):
                store(ch, p * PB + b).start()

    def store(ch, b):
        return pltpu.make_async_copy(
            ob.at[ch, b], out.at[pl.ds(ch * R, R), pl.ds(b * BS, BS)], osem.at[ch, b]
        )

    for b in range(NB):
        load(0, b).wait()
    pl.semaphore_wait(barrier, len(partners))
    for p in range(PIECES):
        send_c(0, 0, p)
    for b in range(NB):
        load(1, b).wait()
    for p in range(PIECES):
        send_c(0, 1, p)

    def weights(m):
        for c in range(NB):
            u = (1 - m) * NB + c
            weight(u).wait()

            @pl.loop(0, 24)
            def _(i, u=u, c=c):
                rs = pl.ds(pl.multiple_of(i * 32, 32), 32)
                x = wst[u, rs, :]
                hi = x.astype(BF16)
                whi[m, c, rs, :] = hi
                wlo[m, c, rs, :] = (x - hi.astype(F32)).astype(BF16)

    every = range(PIECES)
    early, late = every[: PIECES // 2], every[PIECES // 2 :]

    def all_of(f, s, ch, pieces=every):
        for p in pieces:
            f(s, ch, p)

    weights(1)
    weights(0)
    for s in range(STEPS):
        recv_ag(s, 0)
        all_of(kill, s, 0)
        all_of(sums, s, 0, early)
        all_of(forward, s, 0, late)
        recv_ag(s, 1)
        all_of(kill, s, 1)
        all_of(sums, s, 0, late)
        all_of(forward, s, 0, early)
        queue()
        all_of(forward, s, 1, late)
        for p in every:
            comb(s, 0, p)
            if p >= LAG:
                sums(s, 1, p - LAG)
        all_of(sums, s, 1, every[-LAG:])
        all_of(forward, s, 1, early)
        all_of(comb, s, 1)

    for s in range(STEPS):
        for ch in range(CH):
            for p in every:
                for kind in (AG, YA, ZA, YB, ZB, CO):
                    copy(kind, s, ch, p).wait_send()

                first = p < PIECES // 2
                for kind, sender in ((XF, 0 if first else None), (XH, 1 if not first else None)):
                    if sender is None:
                        final_x(s, ch, p, relayed(s, ch, p), d_x3, kind).wait_send()
                    else:
                        @pl.when(xh == sender)
                        def _(s=s, ch=ch, p=p, kind=kind):
                            final_x(s, ch, p, relayed(s, ch, p), d_x3, kind).wait_send()

    for ch in range(CH):
        for b in range(NB):
            store(ch, b).wait()


def local(state, queue_blocks, queue_rows, kill_blocks, kill_rows, rate_index, rate_table):
    buf = lambda *shape: pltpu.VMEM(shape, F32)
    full = (STEPS, CH, NB, R, BS)
    return pl.pallas_call(
        kernel,
        out_shape=jax.ShapeDtypeStruct(state.shape, F32),
        in_specs=[pl.BlockSpec(memory_space=pl.ANY)] * 3
        + [pl.BlockSpec(memory_space=pltpu.SMEM)] * 4,
        out_specs=pl.BlockSpec(memory_space=pl.ANY),
        scratch_shapes=[
            buf(STEPS, CH, 2 * NB, R, BS),
            pltpu.VMEM((2 * NB, 2 * CH * R, BS), BF16),
            buf(*full),
            buf(CH, NB, R, BS),
            buf(*full), buf(*full),
            buf(*full), buf(*full),
            buf(*full), buf(*full),
            buf(*full),
            buf(STEPS, CH, NB // 2, R, BS),
            buf(*full),
            buf(CH, NB, R, BS),
            buf(SLOTS, 3 * BS, BS),
            pltpu.VMEM((2, NB, 3 * BS, BS), BF16),
            pltpu.VMEM((2, NB, 3 * BS, BS), BF16),
            buf(33, 8, BS), buf(6, 8, BS), buf(CH, R // 8, 8, BS),
            pltpu.SemaphoreType.DMA((KINDS, STEPS, CH, PIECES)),
            pltpu.SemaphoreType.DMA((KINDS, STEPS, CH, PIECES)),
            pltpu.SemaphoreType.DMA((SLOTS,)),
            pltpu.SemaphoreType.DMA((CH, NB)),
            pltpu.SemaphoreType.DMA((CH, NB)),
        ],
        compiler_params=pltpu.CompilerParams(
            collective_id=0, has_side_effects=True, vmem_limit_bytes=60 * 1024 * 1024
        ),
        name="chain",
    )(
        state,
        queue_blocks.reshape(NB, 3 * BS, BS),
        kill_blocks.reshape(NB, 3 * BS, BS),
        queue_rows.T, kill_rows.T, rate_index, rate_table.T,
    )


def solution(mesh):
    placed = (
        P("rack", "queue"),
        P("queue", None, None, None),
        P("queue", None),
        P("queue", None, None, None),
        P("queue", None),
        P(),
        P(),
    )
    return jax.shard_map(
        local, mesh=mesh, in_specs=placed, out_specs=P("rack", "queue"), check_vma=False
    )
```
